512 devices in a mesh: row: 32 (over y, x, core), col: 16 (over z).
Axes of the slice: x: 4, y: 4, z: 16, core: 2. Of those that a mesh axis runs over, the one named last changes fastest.
Arguments:
- near_blocks: float32 [32, 16, 512, 512], P('row', 'col'), as said below
- leaf_bases: float32 [32, 512, 512], P('row'), may hold values from -1 to 1, as said below
- upper_bases: float32 [16, 256, 256], P('col'), may hold values from -1 to 1, as said below
- near_list: int32 [32, 16], P('row'), may hold values from 0 to 31, as said below
Outputs:
- factors: float32 [12288, 384], P('row')
- skeleton: float32 [4096, 4096], P('row', 'col')
- upper_skeleton: float32 [2048, 2048], P('row', 'col')
The draws below stay inside these ranges and needn't reach their ends.
Inputs may be any that keep to these rules, and one draw needn't show every extreme that they name: `near_list`: entry 0 of row i is i; every entry of row i lies within 2 of i; entries may repeat. near_blocks[i, k] is the tile between leaf i and leaf near_list[i, k] of a symmetric matrix: a kernel matrix of points, a positive diagonal noise term and independent symmetric random entries; entries naming the same leaf hold equal tiles; every diagonal tile is symmetric positive definite. Each leaf_bases[i] is orthogonal. Each upper_bases[p] is orthogonal.
All inputs are finite; a program needn't handle non-finite values.
Results may differ from the reference program's by a relative error of at most 0.0003.
Values sent between devices are 32-bit elements; how exact they have to be, the bound alone decides.
No kernel may reach another device: no remote copies, remote signals or barrier semaphores. Data moves between devices by JAX's collectives and lax.ppermute only.
A program may use at most 64 MiB of HBM per device.

```python
import math
import jax
import jax.numpy as jnp
from jax import lax

LEAF = 512
SKEL = 128
NEAR = 16
REACH = 2
RED = 384
LEAVES = 32
PARENTS = 16
PARENT = 256


noise_level = 0.015


def orthonormal(key, count, order):
    source = jax.random.normal(key, (count, order, order), jnp.float32)
    ortho, triangle = jnp.linalg.qr(source)
    return ortho


def near_lists(key):
    own_index = jnp.arange(LEAVES, dtype=jnp.int32)[:, None]
    offsets = jax.random.randint(jax.random.fold_in(key, 37), (LEAVES, NEAR), -REACH, REACH + 1)
    listed = jnp.clip(own_index + offsets, 0, LEAVES - 1).astype(jnp.int32)
    column = jnp.arange(NEAR, dtype=jnp.int32)[None, :]
    return jnp.where(column == 0, own_index, listed).astype(jnp.int32)


def leaf_points(key):
    uniforms = jax.random.uniform(jax.random.fold_in(key, 53), (LEAVES, LEAF, 3), jnp.float32)
    across = uniforms[:, :, 0]
    first_coord = jnp.arange(LEAVES, dtype=jnp.float32)[:, None] + across
    return jnp.stack([first_coord, 2.0 * uniforms[:, :, 1], 2.0 * uniforms[:, :, 2]], axis=-1)


def pair_entries(pair_key):
    return jax.random.normal(pair_key, (LEAF, LEAF), jnp.float32)


def symmetric_noise(noise_base, leaf, other):
    forward = pair_entries(jax.random.fold_in(noise_base, leaf * LEAVES + other))
    backward = pair_entries(jax.random.fold_in(noise_base, other * LEAVES + leaf))
    return noise_level / math.sqrt(2.0) * (forward + backward.T)


def draw_near_blocks(key, part):
    listed = near_lists(key)
    points = leaf_points(key)
    noise_key = jax.random.fold_in(key, 61)
    entry_key = jax.random.fold_in(key, 71)
    ridge = jnp.exp(jax.random.uniform(noise_key, (LEAVES, LEAF), jnp.float32, math.log(2.0), math.log(6.0)))
    kernel_scale = 6.0 / LEAF

    def one_leaf(leaf):
        own_points = points[leaf]
        near_points = points[listed[leaf]]
        offsets = own_points[None, :, None, :] - near_points[:, None, :, :]
        distance = jnp.sqrt(jnp.sum(offsets * offsets, axis=-1))
        tiles = kernel_scale * jnp.exp(-distance)
        random_part = jax.vmap(lambda other: symmetric_noise(entry_key, leaf, other))(listed[leaf])
        same_leaf = (listed[leaf] == leaf)[:, None, None]
        return tiles + random_part + jnp.where(same_leaf, jnp.diag(ridge[leaf])[None, :, :], 0.0)
    return lax.map(one_leaf, jnp.arange(LEAVES, dtype=jnp.int32)).astype(jnp.float32)


def draw_leaf_bases(key, part):
    return orthonormal(jax.random.fold_in(key, 11), LEAVES, LEAF)


def draw_upper_bases(key, part):
    return orthonormal(jax.random.fold_in(key, 23), PARENTS, PARENT)


def draw_near_list(key, part):
    return near_lists(key)


def setup_inputs(seed: int = 0) -> dict:
    arg_keys = jax.random.split(jax.random.key(seed), 5)
    near_blocks = draw_near_blocks(jax.random.fold_in(arg_keys[4], 71), 0)
    leaf_bases = draw_leaf_bases(jax.random.fold_in(arg_keys[4], 71), 0)
    upper_bases = draw_upper_bases(jax.random.fold_in(arg_keys[4], 71), 0)
    near_list = draw_near_list(jax.random.fold_in(arg_keys[4], 71), 0)
    return {"near_blocks": near_blocks, "leaf_bases": leaf_bases, "upper_bases": upper_bases, "near_list": near_list}


def product(left, right):
    return jnp.dot(left, right, precision=lax.Precision.HIGHEST)

def lower_solve(factor, rhs):
    return lax.linalg.triangular_solve(factor, rhs, left_side=True, lower=True)

def reference(near_blocks, leaf_bases, upper_bases, near_list):
    leaves = jnp.arange(LEAVES, dtype=jnp.int32)

    def leaf_pivot(col_leaf):
        leaf_basis = leaf_bases[col_leaf]
        rotated = product(product(leaf_basis.T, near_blocks[col_leaf, 0]), leaf_basis)
        factor = jnp.linalg.cholesky(rotated[:RED, :RED])
        return (factor, lower_solve(factor, rotated[:RED, RED:]))
    factor_all, coupling_all = lax.map(leaf_pivot, leaves)

    def leaf_block(row_leaf, col_leaf):
        matches = near_list[row_leaf] == col_leaf
        first_match = jnp.argmax(matches).astype(jnp.int32)

        def live_block(operand):
            near_tile = near_blocks[row_leaf, first_match]
            skel_rows = product(leaf_bases[row_leaf][:, RED:].T, near_tile)
            rotated = product(skel_rows, leaf_bases[col_leaf])
            solved = lower_solve(factor_all[col_leaf], rotated[:, :RED].T)
            return rotated[:, RED:] - product(solved.T, coupling_all[col_leaf])

        def empty_block(operand):
            return jnp.zeros((SKEL, SKEL), jnp.float32)
        return lax.cond(jnp.any(matches), live_block, empty_block, 0)

    def leaf_row(row_leaf):
        return lax.map(lambda col_leaf: leaf_block(row_leaf, col_leaf), leaves)
    blocks = lax.map(leaf_row, leaves)
    skeleton = blocks.transpose(0, 2, 1, 3).reshape(LEAVES * SKEL, LEAVES * SKEL)
    parents = jnp.arange(PARENTS, dtype=jnp.int32)

    def parent_rotated(row_parent, col_parent):
        merged = lax.dynamic_slice(skeleton, (row_parent * PARENT, col_parent * PARENT), (PARENT, PARENT))
        return product(product(upper_bases[row_parent].T, merged), upper_bases[col_parent])

    def parent_pivot(col_parent):
        rotated = parent_rotated(col_parent, col_parent)
        factor = jnp.linalg.cholesky(rotated[:SKEL, :SKEL])
        return (factor, lower_solve(factor, rotated[:SKEL, SKEL:]))
    parent_factors, parent_couplings = lax.map(parent_pivot, parents)

    def parent_block(row_parent, col_parent):
        rotated = parent_rotated(row_parent, col_parent)
        solved = lower_solve(parent_factors[col_parent], rotated[SKEL:, :SKEL].T)
        return rotated[SKEL:, SKEL:] - product(solved.T, parent_couplings[col_parent])

    def parent_row(row_parent):
        return lax.map(lambda col_parent: parent_block(row_parent, col_parent), parents)
    upper_blocks = lax.map(parent_row, parents)
    upper_skeleton = upper_blocks.transpose(0, 2, 1, 3).reshape(PARENTS * SKEL, PARENTS * SKEL)
    return (factor_all.reshape(LEAVES * RED, RED), skeleton, upper_skeleton)
```

```python
import jax
import jax.numpy as jnp
from jax import lax
from jax.experimental import pallas as pl
from jax.experimental.pallas import tpu as pltpu
from jax.sharding import PartitionSpec as P


F32 = jnp.float32
SKEL = 128
RED = 384
REACH = 2
GROUP = 8
ODD_SHIFT = 8
AXES = ("row", "col")
SPREAD = (
    (5, 11, (2, 15, 6, 4, 12, 9), ((0, 1), (2, 3), (6, 7), (9, 8), (11, 10), (12, 13), (15, 14))),
    (5, 11, (2, 15, 6, 4, 12, 9), ((0, 1), (2, 3), (6, 7), (9, 8), (11, 10), (12, 13), (15, 14))),
    (5, 11, (3, 15, 6, 4, 12, 9), ((0, 1), (3, 2), (6, 7), (9, 8), (11, 10), (12, 13), (15, 14))),
    (5, 11, (3, 15, 7, 4, 12, 10), ((0, 1), (3, 2), (5, 6), (7, 8), (10, 9), (12, 13), (15, 14))),
    (6, 11, (4, 15, 7, 5, 12, 10), ((0, 1), (4, 2), (5, 3), (7, 8), (10, 9), (12, 13), (15, 14))),
    (6, 11, (4, 15, 7, 5, 12, 9), ((0, 1), (4, 2), (5, 3), (7, 8), (9, 10), (12, 13), (15, 14))),
    (6, 11, (1, 15, 7, 5, 12, 10), ((1, 2), (5, 3), (6, 4), (7, 8), (10, 9), (12, 13), (15, 14))),
    (6, 10, (1, 15, 7, 5, 12, 9), ((1, 2), (5, 3), (6, 4), (7, 8), (10, 11), (12, 13), (15, 14))),
    (7, 11, (2, 15, 8, 6, 12, 10), ((0, 1), (2, 3), (6, 4), (7, 5), (8, 9), (12, 13), (15, 14))),
    (7, 11, (2, 15, 8, 6, 13, 10), ((0, 1), (2, 3), (6, 4), (7, 5), (8, 9), (11, 12), (13, 14))),
    (7, 11, (1, 15, 8, 3, 12, 10), ((1, 2), (3, 4), (7, 5), (8, 6), (10, 9), (12, 13), (15, 14))),
    (7, 11, (1, 15, 8, 3, 12, 10), ((1, 2), (3, 4), (7, 5), (8, 6), (10, 9), (12, 13), (15, 14))),
    (4, 11, (1, 15, 8, 3, 12, 9), ((1, 2), (4, 5), (8, 6), (9, 7), (11, 10), (12, 13), (15, 14))),
    (4, 11, (1, 15, 8, 3, 12, 9), ((1, 2), (4, 5), (8, 6), (9, 7), (11, 10), (12, 13), (15, 14))),
    (4, 10, (1, 14, 5, 3, 11, 9), ((1, 2), (5, 6), (9, 7), (10, 8), (11, 12), (14, 13), (0, 15))),
    (4, 10, (1, 14, 5, 3, 11, 9), ((1, 2), (5, 6), (9, 7), (10, 8), (11, 12), (14, 13), (0, 15))),
    (5, 11, (1, 15, 6, 4, 12, 10), ((1, 2), (4, 3), (6, 7), (10, 8), (11, 9), (12, 13), (15, 14))),
    (5, 11, (2, 15, 6, 4, 12, 10), ((0, 1), (2, 3), (6, 7), (10, 8), (11, 9), (12, 13), (15, 14))),
    (5, 12, (1, 15, 7, 4, 13, 11), ((1, 2), (4, 3), (5, 6), (7, 8), (11, 9), (12, 10), (13, 14))),
    (5, 12, (2, 15, 7, 4, 13, 11), ((0, 1), (2, 3), (5, 6), (7, 8), (11, 9), (12, 10), (13, 14))),
    (4, 12, (1, 15, 6, 3, 13, 8), ((1, 2), (4, 5), (6, 7), (8, 9), (12, 10), (13, 11), (15, 14))),
    (4, 12, (1, 15, 6, 3, 13, 8), ((1, 2), (4, 5), (6, 7), (8, 9), (12, 10), (13, 11), (15, 14))),
    (5, 13, (1, 15, 7, 4, 14, 9), ((1, 2), (4, 3), (5, 6), (7, 8), (9, 10), (13, 11), (14, 12))),
    (5, 13, (1, 15, 7, 4, 14, 9), ((1, 2), (4, 3), (5, 6), (7, 8), (9, 10), (13, 11), (14, 12))),
    (5, 10, (1, 15, 6, 4, 14, 9), ((1, 2), (4, 3), (6, 7), (9, 8), (10, 11), (14, 12), (15, 13))),
    (5, 10, (1, 15, 6, 3, 14, 9), ((1, 2), (3, 4), (6, 7), (9, 8), (10, 11), (14, 12), (15, 13))),
    (5, 10, (1, 15, 6, 4, 11, 9), ((1, 2), (4, 3), (6, 7), (9, 8), (11, 12), (15, 13), (0, 14))),
    (4, 10, (1, 15, 6, 3, 11, 9), ((1, 2), (4, 5), (6, 7), (9, 8), (11, 12), (15, 13), (0, 14))),
    (3, 9, (1, 12, 4, 2, 10, 7), ((4, 5), (7, 6), (9, 8), (10, 11), (12, 13), (0, 14), (1, 15))),
    (3, 9, (1, 12, 4, 2, 10, 7), ((4, 5), (7, 6), (9, 8), (10, 11), (12, 13), (0, 14), (1, 15))),
    (5, 10, (1, 13, 6, 4, 11, 9), ((1, 2), (4, 3), (6, 7), (9, 8), (11, 12), (13, 14), (0, 15))),
    (5, 10, (1, 13, 6, 4, 11, 9), ((1, 2), (4, 3), (6, 7), (9, 8), (11, 12), (13, 14), (0, 15))),
)


def split(x):
    high = x.astype(jnp.bfloat16)
    return high, (x - high.astype(F32)).astype(jnp.bfloat16)


def three_pass(a, b, dims):
    a_high, a_low = split(a)
    b_high, b_low = split(b)

    def dot(p, q):
        return lax.dot_general(p, q, (dims, ((), ())), preferred_element_type=F32)

    return dot(a_high, b_high) + (dot(a_high, b_low) + dot(a_low, b_high))


def mm(a, b):
    return three_pass(a, b, ((1,), (0,)))


def mtm(a, b):
    return three_pass(a, b, ((0,), (0,)))


def chol_inverse(block):
    n = block.shape[0]
    shape = (GROUP, n)
    sub = lax.broadcasted_iota(jnp.int32, shape, 0)
    lane = lax.broadcasted_iota(jnp.int32, shape, 1)
    groups = n // GROUP
    left = [block[GROUP * g : GROUP * (g + 1)] for g in range(groups)]
    right = [jnp.where(lane == sub + GROUP * g, 1.0, 0.0).astype(F32) for g in range(groups)]
    out_left, out_right = [], []

    def lane_column(rows, column):
        return jnp.broadcast_to(rows[:, column : column + 1], shape)

    def row_of(rows, t):
        return jnp.broadcast_to(rows[t : t + 1], shape)

    for g in range(groups):
        v, e = left[g], right[g]
        columns = [lane_column(v, GROUP * g + t) for t in range(GROUP)]
        scaled_v, scaled_e = v, e
        for t in range(GROUP):
            here = sub == t
            scale = lax.rsqrt(row_of(columns[t], t))
            inverse = scale * scale
            row_v, row_e = row_of(v, t), row_of(e, t)
            scaled_v = jnp.where(here, row_v * scale, scaled_v)
            scaled_e = jnp.where(here, row_e * scale, scaled_e)
            for s in range(t + 1, GROUP):
                q = row_of(columns[s], t) * inverse
                columns[s] = jnp.where(here, q, columns[s] - columns[t] * q)
            q_v, q_e = row_v * inverse, row_e * inverse
            v = jnp.where(here, q_v, v - columns[t] * q_v)
            e = jnp.where(here, q_e, e - columns[t] * q_e)
        out_left.append(scaled_v)
        out_right.append(scaled_e)
        if g + 1 < groups:
            rows_v = [row_of(v, t) for t in range(GROUP)]
            rows_e = [row_of(e, t) for t in range(GROUP)]
            for h in range(g + 1, groups):
                source = left[h]
                new_left, new_right = source, right[h]
                for t in range(GROUP):
                    c = lane_column(source, GROUP * g + t)
                    new_left = new_left - c * rows_v[t]
                    new_right = new_right - c * rows_e[t]
                left[h], right[h] = new_left, new_right
    upper = jnp.concatenate(out_left, axis=0)
    inverse = jnp.concatenate(out_right, axis=0)
    r = lax.broadcasted_iota(jnp.int32, (n, n), 0)
    c = lax.broadcasted_iota(jnp.int32, (n, n), 1)
    return jnp.where(c >= r, upper, 0.0), jnp.where(c <= r, inverse, 0.0)


def home_col(i):
    z = ((i >> 1) + ODD_SHIFT * (i & 1)) & 15
    if isinstance(i, int):
        return z or 1
    return jnp.where(z == 0, 1, z)


def flat(i, z):
    return i * 16 + z


def send(value, pairs):
    return lax.ppermute(value, AXES, [p for p in pairs if p[0] != p[1]])


def spread_rounds(i):
    first, second, middle, last = SPREAD[i]
    seeds = (0, first, second)
    hops = [(seeds[n // 2], z) for n, z in enumerate(middle)]
    return [[(0, first)], [(0, second)], hops[0::2], hops[1::2], list(last)]


def pivot_kernel(near_ref, basis_ref, part_ref, pack_ref, wide_ref):
    col = lax.axis_index("col")

    @pl.when(col != 0)
    def _():
        part_ref[...] = mtm(basis_ref[:, RED:], near_ref[...])
        pack_ref[...] = jnp.zeros_like(pack_ref)

    @pl.when(col == 0)
    def _():
        basis = basis_ref[...]
        right = mm(near_ref[...], basis)
        rotated = mtm(basis[:, :RED], right)
        basis_t = basis[:, :RED].T
        rows = [
            jnp.concatenate([rotated[128 * b : 128 * b + 128], basis_t[128 * b : 128 * b + 128]], axis=1)
            for b in range(3)
        ]
        wide = basis[:, RED:]
        place = 0
        for b in range(3):
            upper, inverse = chol_inverse(rows[b][:, 128 * b : 128 * b + 128])
            solved = mm(inverse, rows[b][:, 128 * (b + 1) :])
            pack_ref[128 * place : 128 * place + 128] = upper.T
            place += 1
            for c in range(b + 1, 3):
                above = solved[:, 128 * (c - b - 1) : 128 * (c - b)]
                pack_ref[128 * place : 128 * place + 128] = above.T
                place += 1
                rows[c] = jnp.concatenate(
                    [rows[c][:, : 128 * (b + 1)], rows[c][:, 128 * (b + 1) :] - mtm(above, solved)], axis=1
                )
            offset = 128 * (2 - b)
            wide = wide - mtm(solved[:, offset + 128 :], solved[:, offset : offset + 128])
        wide_ref[...] = wide
        part_ref[:, :SKEL] = mtm(right[:, RED:], wide)


def pivot(near_tile, basis):
    return pl.pallas_call(
        pivot_kernel,
        out_shape=[
            jax.ShapeDtypeStruct((SKEL, 512), F32),
            jax.ShapeDtypeStruct((6 * 128, 128), F32),
            jax.ShapeDtypeStruct((512, SKEL), F32),
        ],
        cost_estimate=pl.CostEstimate(flops=2_000_000_000, bytes_accessed=4_000_000, transcendentals=0),
        name="pivot",
    )(near_tile, basis)


def tiles_kernel(near_ref, *refs):
    wide_refs, part_refs = refs[:4], refs[4:20]
    piece_refs, strip_ref, (buffer, chosen, sems) = refs[20:23], refs[23], refs[24:]
    row, col = lax.axis_index("row"), lax.axis_index("col")
    home = home_col(row)

    @pl.when(col == home)
    def _():
        for d in range(5):
            chosen[d] = -1
        for k in range(15, -1, -1):
            chosen[near_ref[0, k] - row + REACH] = k
        slot = row & 1
        for piece in piece_refs:
            piece[...] = jnp.zeros_like(piece)
        strip_ref[...] = jnp.zeros_like(strip_ref)

        def put(d, value):
            for s in range(2):
                place = d + s

                @pl.when(slot == s)
                def _():
                    lanes = slice(128 * (place % 2), 128 * (place % 2) + 128)
                    piece_refs[place // 2][:, lanes] = value
                    strip_ref[place // 2, :, lanes] = value

        for d in range(5):
            k = chosen[d]
            step = (k - home) & 15
            for r in range(16):

                @pl.when((k >= 0) & (step == r))
                def _():
                    pltpu.make_async_copy(part_refs[r], buffer.at[d], sems.at[d]).start()

        for d in range(5):

            @pl.when(chosen[d] >= 0)
            def _():
                pltpu.make_async_copy(part_refs[0], buffer.at[d], sems.at[d]).wait()
                if d == REACH:
                    put(d, buffer[d, :, :SKEL])
                else:
                    put(d, mm(buffer[d], wide_refs[d - (d > REACH)][...]))


def finish_tiles(near_row, wides, parts):
    any_spec = pl.BlockSpec(memory_space=pl.ANY)
    vmem = pl.BlockSpec(memory_space=pltpu.VMEM)
    return pl.pallas_call(
        tiles_kernel,
        out_shape=[jax.ShapeDtypeStruct((SKEL, 2 * SKEL), F32)] * 3
        + [jax.ShapeDtypeStruct((3, SKEL, 2 * SKEL), F32)],
        in_specs=[pl.BlockSpec(memory_space=pltpu.SMEM)] + [vmem] * 4 + [any_spec] * 16,
        out_specs=[vmem] * 4,
        scratch_shapes=[
            pltpu.VMEM((5, SKEL, 512), F32),
            pltpu.SMEM((5,), jnp.int32),
            pltpu.SemaphoreType.DMA((5,)),
        ],
        cost_estimate=pl.CostEstimate(flops=300_000_000, bytes_accessed=2_000_000, transcendentals=0),
        name="finish_tiles",
    )(near_row, *wides, *parts)


def in_order(slot, own, other):
    return jnp.where(slot == 0, jnp.concatenate([own, other], axis=0), jnp.concatenate([other, own], axis=0))


def half_columns(slot, basis):
    return jnp.where(slot == 0, basis[:, SKEL : SKEL + 64], basis[:, SKEL + 64 :])


def home_basis(row, col, basis_ref, moved_ref):
    return jnp.where(col == row >> 1, basis_ref[...], moved_ref[...])


def parent_kernel(own_ref, other_ref, basis_ref, moved_ref, narrow_ref, middle_ref):
    row, col = lax.axis_index("row"), lax.axis_index("col")
    slot = row & 1

    @pl.when(col == home_col(row))
    def _():
        merged = in_order(slot, own_ref[1], other_ref[1])
        basis = home_basis(row, col, basis_ref, moved_ref)
        left = mtm(basis[:, :SKEL], merged)
        rotated = mm(left, basis)
        block = rotated[:, :SKEL]
        _, inverse = chol_inverse((block + block.T) * 0.5)
        coupled = mtm(inverse, mm(inverse, rotated[:, SKEL:]))
        narrow = basis[:, SKEL:] - mm(basis[:, :SKEL], coupled)
        narrow_ref[...] = narrow
        middle_ref[...] = mm(mtm(half_columns(slot, basis), merged), narrow)


def parent(*operands):
    return pl.pallas_call(
        parent_kernel,
        out_shape=[
            jax.ShapeDtypeStruct((2 * SKEL, SKEL), F32),
            jax.ShapeDtypeStruct((SKEL // 2, SKEL), F32),
        ],
        cost_estimate=pl.CostEstimate(flops=500_000_000, bytes_accessed=1_000_000, transcendentals=0),
        name="parent",
    )(*operands)


def outer_kernel(own_ref, other_ref, basis_ref, moved_ref, low_ref, high_ref, out_low, out_high):
    row, col = lax.axis_index("row"), lax.axis_index("col")
    slot = row & 1

    @pl.when(col == home_col(row))
    def _():
        basis = half_columns(slot, home_basis(row, col, basis_ref, moved_ref))
        low = in_order(slot, own_ref[0], other_ref[0])
        high = in_order(slot, own_ref[2], other_ref[2])
        out_low[...] = mm(mtm(basis, low), low_ref[...])
        out_high[...] = mm(mtm(basis, high), high_ref[...])


def outer(*operands):
    return pl.pallas_call(
        outer_kernel,
        out_shape=[jax.ShapeDtypeStruct((SKEL // 2, SKEL), F32)] * 2,
        cost_estimate=pl.CostEstimate(flops=100_000_000, bytes_accessed=1_000_000, transcendentals=0),
        name="outer",
    )(*operands)


LEAVES = range(32)


def beside(value, distance):
    distances = distance if callable(distance) else lambda i: distance
    pairs = []
    for i in LEAVES:
        t = i + distances(i)
        if t in LEAVES:
            pairs.append((flat(i, home_col(i)), flat(t, home_col(t))))
    return send(value, pairs)


def place(values, at_home, shift):
    total = None
    for e in (-1, 0, 1):
        pairs = [
            (flat(i, home_col(i)), flat(i, i // 2 + e)) for i in LEAVES if 0 <= i // 2 + e < 16
        ]
        got = send(values[e + 1], pairs)
        total = got if total is None else total + got
    mine = jnp.where(shift == -1, values[0], jnp.where(shift == 0, values[1], values[2]))
    return jnp.where(at_home & (jnp.abs(shift) <= 1), mine, total)


def local(near_blocks, leaf_bases, upper_bases, near_list):
    return step(near_blocks[0, 0], leaf_bases[0], upper_bases[0], near_list)


def step(near_tile, leaf_basis, upper_basis, near_row):
    row, col = lax.axis_index("row"), lax.axis_index("col")
    at_home = col == home_col(row)
    shift = col - (row >> 1)

    part, pack, wide = pivot(near_tile, leaf_basis)

    wides = []
    for d in (-2, -1, 1, 2):
        pairs = [(flat(i + d, 0), flat(i, home_col(i))) for i in LEAVES if i + d in LEAVES]
        wides.append(send(wide, pairs))

    parts = [part] * 16
    for r in range(1, 16):
        pairs = [(flat(i, (home_col(i) + r) % 16), flat(i, home_col(i))) for i in LEAVES]
        parts[r] = send(part, pairs)

    held = pack
    for wave in ((0, 1), (2, 3), (4,)):
        got = []
        for n in wave:
            pairs = [(flat(i, a), flat(i, b)) for i in LEAVES for a, b in spread_rounds(i)[n]]
            got.append(send(held, pairs))
        held = sum(got, held)

    moved = send(upper_basis, [(flat(i, i // 2), flat(i, home_col(i))) for i in LEAVES])

    *pieces, strip = finish_tiles(near_row, wides, parts)
    other = beside(strip, lambda i: -1 if i % 2 else 1)
    narrow, middle = parent(strip, other, upper_basis, moved)
    narrow_low = beside(narrow, 2)
    narrow_high = beside(narrow, -2)
    up_low, up_high = outer(strip, other, upper_basis, moved, narrow_low, narrow_high)

    skeleton = place(pieces, at_home, shift)
    upper = place([up_low, middle, up_high], at_home, shift)

    blocks = [held[128 * n : 128 * n + 128] for n in range(6)]
    zero = jnp.zeros((128, 128), F32)
    factor = jnp.concatenate(
        [
            jnp.concatenate([blocks[0], zero, zero], axis=1),
            jnp.concatenate([blocks[1], blocks[3], zero], axis=1),
            jnp.concatenate([blocks[2], blocks[4], blocks[5]], axis=1),
        ],
        axis=0,
    )
    return factor, skeleton, upper


def solution(mesh):
    return jax.shard_map(
        local,
        mesh=mesh,
        in_specs=(
            P("row", "col", None, None),
            P("row", None, None),
            P("col", None, None),
            P("row", None),
        ),
        out_specs=(P("row", None), P("row", "col"), P("row", "col")),
        check_vma=False,
    )
```
